32 devices in a mesh: row: 2 (over x), col: 4 (over y, core), layer: 4 (over z).
Axes of the slice: x: 2, y: 2, z: 4, core: 2. Of those that a mesh axis runs over, the one named last changes fastest.
Arguments:
- flow_matrix: float32 [2048, 2048], P('row', ('layer', 'col')), may hold values from 0.0009 to 310, as said below
- regularizer: float32 [2048, 2048], P(('layer', 'row'), 'col'), may hold values from 0.001 to 1
- pattern: int32 [8, 8], replicated, may hold values from 0 to 1, as said below
Outputs:
- inflated: float32 [2048, 2048], P(('row', 'layer'), 'col')
The draws below stay inside these ranges and needn't reach their ends.
Inputs may be any that keep to these rules, and one draw needn't show every extreme that they name: `flow_matrix`: entries are positive. `pattern`: each entry is 0 or 1; every diagonal entry is 1.
All inputs are finite; a program needn't handle non-finite values.
Results may differ from the reference program's by a relative error of at most 0.000098.
Values sent between devices are 32-bit elements; how exact they have to be, the bound alone decides.
No kernel may reach another device: no remote copies, remote signals or barrier semaphores. Data moves between devices by JAX's collectives and lax.ppermute only.
A program may use at most 64 MiB of HBM per device.

```python
import math
import jax
import jax.numpy as jnp
from jax import lax

TILE = 256
GRID = 8
N = 2048


def draw_flow_matrix(key, part):
    keys = jax.random.split(jax.random.fold_in(key, 11), 3)
    entries = jnp.exp(jax.random.uniform(keys[0], (N, N), jnp.float32, jnp.log(0.001), 0.0))
    position = jnp.arange(N, dtype=jnp.float32) / N
    row_scale = 10.0 ** jax.random.uniform(keys[1], (N,), jnp.float32) * jnp.exp(1.1 * position)
    col_scale = 10.0 ** jax.random.uniform(keys[2], (N,), jnp.float32)
    return entries * row_scale[:, None] * col_scale[None, :]


def draw_pattern(key, part):
    coins = jax.random.randint(jax.random.fold_in(key, 23), (GRID, GRID), 0, 2)
    diagonal = (jnp.arange(GRID)[:, None] == jnp.arange(GRID)[None, :]).astype(jnp.int32)
    return jnp.maximum(coins, diagonal).astype(jnp.int32)


def level_of(rng, dims, cuts, smallest, largest):
    level = 1.0
    for dim, shards_of in cuts:
        steps = jax.random.uniform(jax.random.fold_in(jax.random.fold_in(rng, 6), dim), (shards_of,), jnp.float32, smallest / len(cuts), largest / len(cuts))
        level = level * jnp.repeat(jnp.exp(steps), dims[dim] // shards_of).reshape((-1,) + (1,) * (len(dims) - 1 - dim))
    return level


def setup_inputs(seed: int = 0) -> dict:
    key_list = jax.random.split(jax.random.key(seed), 4)
    return {
        "flow_matrix": draw_flow_matrix(jax.random.fold_in(key_list[3], 71), 0),
        "regularizer": jnp.clip(jnp.exp(math.log(1.0) - 6.9077552 * jax.random.uniform(key_list[1], (N, N), jnp.float32) ** level_of(key_list[1], (N, N), ((0, 8), (1, 4)), -0.2, 0.2)), 0.001, 1.0),
        "pattern": draw_pattern(jax.random.fold_in(key_list[3], 71), 0),
    }


def reference(flow_matrix, regularizer, pattern):
    expanded = jnp.dot(flow_matrix, regularizer, precision=lax.Precision.HIGHEST, preferred_element_type=jnp.float32)
    tiled = expanded.reshape(GRID, TILE, GRID, TILE)
    pruned = (tiled * pattern.astype(jnp.float32)[:, None, :, None]).reshape(N, N)
    squared = pruned * pruned
    totals = jnp.sum(squared, axis=0)
    return squared / totals[None, :] * N
```

```python
import jax
import jax.numpy as jnp
from jax import lax
from jax.sharding import PartitionSpec as P


def bits_of(count):
    bits, bit = [], 1
    while bit < count:
        bits.append(bit)
        bit *= 2
    return bits[::-1]


def swap(value, axis, bit):
    return lax.ppermute(value, axis, [(i, i ^ bit) for i in range(lax.axis_size(axis))])


def far_pieces(value, axis, skip):
    pieces = {0: value}
    for bit in bits_of(lax.axis_size(axis)):
        if bit > skip:
            for j in list(pieces):
                pieces[j ^ bit] = swap(pieces[j], axis, bit)
    del pieces[0]
    return pieces


def in_order(pieces, axis, dim):
    index = lax.axis_index(axis)
    blocks = [pieces[j] for j in range(len(pieces))]
    for bit in bits_of(len(pieces)):
        flip = (index & bit) != 0
        blocks = [jnp.where(flip, blocks[j ^ bit], blocks[j]) for j in range(len(blocks))]
    return jnp.concatenate(blocks, axis=dim)


def total_over(value, axis):
    for bit in bits_of(lax.axis_size(axis))[::-1]:
        value = value + swap(value, axis, bit)
    return value


def kept_tiles(pattern, row_start, row_count, col_start, col_count, tile):
    ids = lax.iota(jnp.int32, pattern.shape[0])
    row_tile = (row_start + lax.iota(jnp.int32, row_count)) // tile
    col_tile = (col_start + lax.iota(jnp.int32, col_count)) // tile
    row_pick = (row_tile[:, None] == ids[None, :]).astype(jnp.float32)
    col_pick = (ids[:, None] == col_tile[None, :]).astype(jnp.float32)
    return jnp.dot(jnp.dot(row_pick, pattern.astype(jnp.float32)), col_pick)


def exchange(value, targets):
    return lax.ppermute(value, "layer", list(enumerate(targets)))


def shards(flow_matrix, regularizer, pattern):
    row_count, layer_count = lax.axis_size("row"), lax.axis_size("layer")
    order_total = flow_matrix.shape[0] * row_count
    tile = order_total // pattern.shape[0]
    rows, width = flow_matrix.shape[0], regularizer.shape[1]
    own, part = rows // layer_count, width // 2
    row, col, layer = (lax.axis_index(a) for a in ("row", "col", "layer"))
    last = layer_count - 1
    end = (layer == 0) | (layer == last)

    def blocks_of(values, offsets):
        blocks = [lax.dynamic_slice_in_dim(values, (layer ^ k) * own, own, 0) for k in offsets]
        return jnp.concatenate(blocks, axis=0)

    near = swap(flow_matrix, "col", 1)

    def gather_left(offsets):
        mine = blocks_of(flow_matrix, offsets)
        pieces = far_pieces(mine, "col", 1)
        for j in list(pieces):
            pieces[j ^ 1] = swap(pieces[j], "col", 1)
        pieces.update({0: mine, 1: blocks_of(lax.optimization_barrier(near), offsets)})
        return in_order(lax.optimization_barrier(pieces), "col", 1)

    def gather_right(value):
        pieces = far_pieces(value, "row", 0)
        pieces[0] = value
        return in_order(pieces, "row", 0)

    first = gather_left((2, 3))
    rest = gather_left((1, 0))
    rights = [gather_right(lax.optimization_barrier(regularizer[:, h * part:(h + 1) * part])) for h in range(2)]

    def product(left, right):
        value = jnp.dot(
            left, right, precision=lax.Precision.HIGH, preferred_element_type=jnp.float32
        )
        return lax.optimization_barrier(value)

    kept = kept_tiles(pattern, row * rows + layer * own, own, col * width, width, tile)
    relay = (1, last, 0, last - 1)
    right = jnp.concatenate(rights, axis=1)
    seconds = [exchange(product(first[:own], rights[h]), relay) for h in range(2)]
    third = product(first[own:], right)
    across = lax.ppermute(third, "layer", [(0, last), (last, 0)])
    others = product(rest, right)
    beside = swap(others[:own], "layer", 1)
    seconds = jnp.concatenate(seconds, axis=1)
    passed = lax.ppermute(third + seconds, "layer", [(1, 2), (2, 1)])
    expanded = others[own:] + beside + across + passed + jnp.where(end, seconds, 0.0)
    pruned = expanded * kept
    squared = pruned * pruned
    totals = jnp.sum(squared, axis=0, keepdims=True)
    totals = total_over(total_over(totals, "row"), "layer")
    return squared / totals * order_total


def solution(mesh):
    return jax.shard_map(
        shards,
        mesh=mesh,
        in_specs=(P("row", ("layer", "col")), P(("layer", "row"), "col"), P()),
        out_specs=P(("row", "layer"), "col"),
        check_vma=False,
    )
```

```python
import jax
import jax.numpy as jnp
from jax import lax
from jax.sharding import PartitionSpec as P


def bits_of(count):
    bits, bit = [], 1
    while bit < count:
        bits.append(bit)
        bit *= 2
    return bits[::-1]


def swap(value, axis, bit):
    return lax.ppermute(value, axis, [(i, i ^ bit) for i in range(lax.axis_size(axis))])


def far_pieces(value, axis, skip):
    pieces = {0: value}
    for bit in bits_of(lax.axis_size(axis)):
        if bit > skip:
            for j in list(pieces):
                pieces[j ^ bit] = swap(pieces[j], axis, bit)
    del pieces[0]
    return pieces


def flipped(blocks, mask):
    for bit in bits_of(len(blocks)):
        flip = (mask & bit) != 0
        blocks = [jnp.where(flip, blocks[j ^ bit], blocks[j]) for j in range(len(blocks))]
    return blocks


def total_over(value, axis):
    for bit in bits_of(lax.axis_size(axis))[::-1]:
        value = value + swap(value, axis, bit)
    return value


def kept_tiles(pattern, row_start, row_count, col_start, col_count, tile):
    ids = lax.iota(jnp.int32, pattern.shape[0])
    row_tile = (row_start + lax.iota(jnp.int32, row_count)) // tile
    col_tile = (col_start + lax.iota(jnp.int32, col_count)) // tile
    row_pick = (row_tile[:, None] == ids[None, :]).astype(jnp.float32)
    col_pick = (ids[:, None] == col_tile[None, :]).astype(jnp.float32)
    return jnp.dot(jnp.dot(row_pick, pattern.astype(jnp.float32)), col_pick)


def exchange(value, targets):
    return lax.ppermute(value, "layer", list(enumerate(targets)))


def shards(flow_matrix, regularizer, pattern):
    row_count, layer_count = lax.axis_size("row"), lax.axis_size("layer")
    order_total = flow_matrix.shape[0] * row_count
    tile = order_total // pattern.shape[0]
    rows, width = flow_matrix.shape[0], regularizer.shape[1]
    own, part = rows // layer_count, width // 2
    row, col, layer = (lax.axis_index(a) for a in ("row", "col", "layer"))
    last = layer_count - 1
    end = (layer == 0) | (layer == last)

    def blocks_of(values, offsets):
        blocks = [lax.dynamic_slice_in_dim(values, (layer ^ k) * own, own, 0) for k in offsets]
        return jnp.concatenate(blocks, axis=0)

    near = swap(flow_matrix, "col", 1)

    def gather_left(offsets):
        mine = blocks_of(flow_matrix, offsets)
        pieces = far_pieces(mine, "col", 1)
        for j in list(pieces):
            pieces[j ^ 1] = swap(pieces[j], "col", 1)
        pieces.update({0: mine, 1: blocks_of(lax.optimization_barrier(near), offsets)})
        return pieces

    def left_blocks(pieces, count, *earlier):
        pieces, _ = lax.optimization_barrier((pieces, earlier))
        return [
            jnp.concatenate([pieces[j][k * own:(k + 1) * own] for j in range(len(pieces))], axis=1)
            for k in range(count)
        ]

    shared = lax.axis_size("col") // row_count
    mask = (row ^ (col // shared)) * shared + col % shared

    def gather_right(value):
        pieces = far_pieces(value, "row", 0)
        pieces[0] = value
        depth = value.shape[0] // shared
        blocks = [
            pieces[i][k * depth:(k + 1) * depth] for i in range(row_count) for k in range(shared)
        ]
        return jnp.concatenate(flipped(blocks, mask), axis=0)

    first, second, rest = (
        gather_left(offsets)
        for offsets in ((2,), (3,), (1, 0))
    )
    halves = [lax.optimization_barrier(regularizer[:, h * part:(h + 1) * part]) for h in range(2)]
    rights = [gather_right(halves[h]) for h in range(2)]
    ahead_right = gather_right(swap(halves[1], "layer", 1))
    ahead = swap(blocks_of(flow_matrix, (1,)), "layer", 1)
    ahead = far_pieces(ahead, "col", 1) | {0: ahead}
    ahead.update({j ^ 1: swap(ahead[j], "col", 1) for j in list(ahead)})

    def product(left, right):
        value = jnp.dot(
            left, right, precision=lax.Precision.HIGH, preferred_element_type=jnp.float32
        )
        return lax.optimization_barrier(value)

    kept = kept_tiles(pattern, row * rows + layer * own, own, col * width, width, tile)
    relay = (1, last, 0, last - 1)
    inward = [(0, 1), (last, last - 1)]
    (first,) = left_blocks(first, 1)
    heads = [product(first, rights[h]) for h in range(2)]
    (second,) = left_blocks(second, 1, heads[0])
    thirds = [product(second, rights[h]) for h in range(2)]
    rest, _ = lax.optimization_barrier((rest, thirds[0]))
    rest = jnp.concatenate([rest[j] for j in range(len(rest))], axis=1)
    fourth = product(rest, rights[0])
    mine = product(rest[own:], rights[1])
    ahead, kept = lax.optimization_barrier((ahead, kept, fourth))[:2]
    (ahead,) = left_blocks(ahead, 1)
    mine = mine + product(ahead, ahead_right)
    hop_1 = exchange(heads[0], relay)
    hop_2 = lax.ppermute(thirds[1], "layer", inward)
    hop_3 = exchange(heads[1] + hop_2, relay)
    hop_4 = swap(thirds[0] + jnp.where(end, 0.0, hop_1), "layer", last)
    hop_5 = swap(fourth[:own], "layer", 1)
    hop_6 = lax.ppermute(thirds[1] + hop_3, "layer", [(1, 2), (2, 1)])
    results = [
        fourth[own:] + hop_5 + hop_4 + jnp.where(end, hop_1, 0.0),
        mine + hop_6 + jnp.where(end, hop_3, 0.0),
    ]
    expanded = jnp.concatenate(results, axis=1)
    pruned = expanded * kept
    squared = pruned * pruned
    totals = jnp.sum(squared, axis=0, keepdims=True)
    totals = total_over(total_over(totals, "row"), "layer")
    return squared / totals * order_total


def solution(mesh):
    return jax.shard_map(
        shards,
        mesh=mesh,
        in_specs=(P("row", ("layer", "col")), P(("layer", "row"), "col"), P()),
        out_specs=P(("row", "layer"), "col"),
        check_vma=False,
    )
```

```python
import jax
import jax.numpy as jnp
from jax import lax
from jax.sharding import PartitionSpec as P


def bits_of(count):
    bits, bit = [], 1
    while bit < count:
        bits.append(bit)
        bit *= 2
    return bits[::-1]


def swap(value, axis, bit):
    return lax.ppermute(value, axis, [(i, i ^ bit) for i in range(lax.axis_size(axis))])


def far_pieces(value, axis, skip):
    pieces = {0: value}
    for bit in bits_of(lax.axis_size(axis)):
        if bit > skip:
            for j in list(pieces):
                pieces[j ^ bit] = swap(pieces[j], axis, bit)
    del pieces[0]
    return pieces


def flipped(blocks, mask):
    for bit in bits_of(len(blocks)):
        flip = (mask & bit) != 0
        blocks = [jnp.where(flip, blocks[j ^ bit], blocks[j]) for j in range(len(blocks))]
    return blocks


def total_over(value, axis):
    count = lax.axis_size(axis)
    for bit in [count - 1] + bits_of(count)[1:]:
        value = value + swap(value, axis, bit)
    return value


def kept_tiles(pattern, row_start, row_count, col_start, col_count, tile):
    ids = lax.iota(jnp.int32, pattern.shape[0])
    row_tile = (row_start + lax.iota(jnp.int32, row_count)) // tile
    col_tile = (col_start + lax.iota(jnp.int32, col_count)) // tile
    row_pick = (row_tile[:, None] == ids[None, :]).astype(jnp.float32)
    col_pick = (ids[:, None] == col_tile[None, :]).astype(jnp.float32)
    return jnp.dot(jnp.dot(row_pick, pattern.astype(jnp.float32)), col_pick)


def exchange(value, targets):
    return lax.ppermute(value, "layer", list(enumerate(targets)))


def shards(flow_matrix, regularizer, pattern):
    row_count, layer_count = lax.axis_size("row"), lax.axis_size("layer")
    order_total = flow_matrix.shape[0] * row_count
    tile = order_total // pattern.shape[0]
    rows, width = flow_matrix.shape[0], regularizer.shape[1]
    own, part = rows // layer_count, width // 2
    row, col, layer = (lax.axis_index(a) for a in ("row", "col", "layer"))
    last = layer_count - 1
    end = (layer == 0) | (layer == last)

    def blocks_of(values, offsets):
        blocks = [lax.dynamic_slice_in_dim(values, (layer ^ k) * own, own, 0) for k in offsets]
        return jnp.concatenate(blocks, axis=0)

    near = swap(flow_matrix, "col", 1)

    def gather_left(offsets):
        mine = blocks_of(flow_matrix, offsets)
        pieces = far_pieces(mine, "col", 1)
        for j in list(pieces):
            pieces[j ^ 1] = swap(pieces[j], "col", 1)
        pieces.update({0: mine, 1: blocks_of(lax.optimization_barrier(near), offsets)})
        return pieces

    def left_blocks(pieces, count, *earlier):
        pieces, _ = lax.optimization_barrier((pieces, earlier))
        return [
            jnp.concatenate([pieces[j][k * own:(k + 1) * own] for j in range(len(pieces))], axis=1)
            for k in range(count)
        ]

    shared = lax.axis_size("col") // row_count
    mask = (row ^ (col // shared)) * shared + col % shared

    def gather_right(value):
        pieces = far_pieces(value, "row", 0)
        pieces[0] = value
        depth = value.shape[0] // shared
        blocks = [
            pieces[i][k * depth:(k + 1) * depth] for i in range(row_count) for k in range(shared)
        ]
        return jnp.concatenate(flipped(blocks, mask), axis=0)

    first, second, rest = (
        gather_left(offsets)
        for offsets in ((2,), (3,), (1, 0))
    )
    halves = [lax.optimization_barrier(regularizer[:, h * part:(h + 1) * part]) for h in range(2)]
    rights = [gather_right(halves[h]) for h in range(2)]
    ahead_right = gather_right(swap(halves[1], "layer", 1))
    ahead = swap(blocks_of(flow_matrix, (1,)), "layer", 1)
    ahead = far_pieces(ahead, "col", 1) | {0: ahead}
    ahead.update({j ^ 1: swap(ahead[j], "col", 1) for j in list(ahead)})

    def product(left, right):
        value = jnp.dot(
            left, right, precision=lax.Precision.HIGH, preferred_element_type=jnp.float32
        )
        return lax.optimization_barrier(value)

    kept_rows = own if tile % own else 1
    kept = kept_tiles(pattern, row * rows + layer * own, kept_rows, col * width, width, tile)
    relay = (1, last, 0, last - 1)
    inward = [(0, 1), (last, last - 1)]
    middle, outward = [(1, 2), (2, 1)], [(1, last), (2, 0)]
    (first,) = left_blocks(first, 1)
    heads = [product(first, rights[h]) for h in range(2)]
    (second,) = left_blocks(second, 1, heads[0])
    thirds = [product(second, rights[h]) for h in range(2)]
    rest, _ = lax.optimization_barrier((rest, thirds[0]))
    rest = jnp.concatenate([rest[j] for j in range(len(rest))], axis=1)
    fourth = product(rest, rights[0])
    mine = product(rest[own:], rights[1])
    ahead, kept = lax.optimization_barrier((ahead, kept, fourth))[:2]
    (ahead,) = left_blocks(ahead, 1)
    mine = mine + product(ahead, ahead_right)
    hop_1 = exchange(heads[0], relay)
    hop_2 = lax.ppermute(thirds[1], "layer", inward)
    hop_3 = lax.ppermute(heads[1], "layer", inward)
    hop_4 = swap(thirds[0] + jnp.where(end, 0.0, hop_1), "layer", last)
    hop_5 = swap(fourth[:own], "layer", 1)
    hop_6 = lax.ppermute(thirds[1] + hop_3, "layer", middle)
    hop_7 = lax.ppermute(heads[1] + hop_2, "layer", outward)
    results = [
        fourth[own:] + hop_5 + hop_4 + jnp.where(end, hop_1, 0.0),
        mine + hop_6 + hop_7,
    ]
    expanded = jnp.concatenate(results, axis=1)
    pruned = expanded * kept
    squared = pruned * pruned
    totals = jnp.sum(squared, axis=0, keepdims=True)
    totals = total_over(total_over(totals, "row"), "layer")
    return squared / totals * order_total


def solution(mesh):
    return jax.shard_map(
        shards,
        mesh=mesh,
        in_specs=(P("row", ("layer", "col")), P(("layer", "row"), "col"), P()),
        out_specs=P(("row", "layer"), "col"),
        check_vma=False,
    )
```
